128 devices in a mesh: dp: 8 (over x, core), fsdp: 16 (over z, y).
Axes of the slice: x: 4, y: 4, z: 4, core: 2. Of those that a mesh axis runs over, the one named last changes fastest.
Arguments:
- images: bfloat16 [256, 196, 512], P(('dp', 'fsdp')), may hold values from -6 to 6
- cotangent: bfloat16 [256, 196, 512], P(('dp', 'fsdp')), may hold values from -24 to 24
- counts: int32 [128], P(('dp', 'fsdp')), may hold values from 1 to 2, as said below
- rel_index: int32 [49, 49], replicated, may hold values from 0 to 168, as said below
- region_ids: int32 [196], replicated, may hold values from 0 to 8, as said below
- qkv_weight: bfloat16 [2, 512, 1536], P(None, 'fsdp'), may hold values from -0.25 to 0.25
- qv_bias: bfloat16 [2, 1024], P(None, 'fsdp'), may hold values from -3 to 3
- proj_weight: bfloat16 [2, 512, 512], P(None, 'fsdp'), may hold values from -1 to 1
- proj_bias: bfloat16 [2, 512], P(None, 'fsdp'), may hold values from -3 to 3
- fc1_weight: bfloat16 [2, 512, 2048], P(None, 'fsdp'), may hold values from -0.25 to 0.25
- fc1_bias: bfloat16 [2, 2048], P(None, 'fsdp'), may hold values from -3 to 3
- fc2_weight: bfloat16 [2, 2048, 512], P(None, 'fsdp'), may hold values from -0.125 to 0.125
- fc2_bias: bfloat16 [2, 512], P(None, 'fsdp'), may hold values from -3 to 3
- norm_gains: bfloat16 [2, 2, 512], P(None, None, 'fsdp'), may hold values from 0.5 to 1.5
- norm_biases: bfloat16 [2, 2, 512], P(None, None, 'fsdp'), may hold values from -3 to 3
- rel_table: bfloat16 [2, 169, 16], P(None, None, 'fsdp'), may hold values from -4 to 354
Outputs:
- activations: float32 [256, 196, 512], P(('dp', 'fsdp'))
- images_grad: float32 [256, 196, 512], P(('dp', 'fsdp'))
- qkv_weight_grad: float32 [2, 512, 1536], P(None, 'fsdp')
- qv_bias_grad: float32 [2, 1024], P(None, 'fsdp')
- proj_weight_grad: float32 [2, 512, 512], P(None, 'fsdp')
- proj_bias_grad: float32 [2, 512], P(None, 'fsdp')
- fc1_weight_grad: float32 [2, 512, 2048], P(None, 'fsdp')
- fc1_bias_grad: float32 [2, 2048], P(None, 'fsdp')
- fc2_weight_grad: float32 [2, 2048, 512], P(None, 'fsdp')
- fc2_bias_grad: float32 [2, 512], P(None, 'fsdp')
- norm_gains_grad: float32 [2, 2, 512], P(None, None, 'fsdp')
- norm_biases_grad: float32 [2, 2, 512], P(None, None, 'fsdp')
- rel_table_grad: float32 [2, 169, 16], P(None, None, 'fsdp')
The draws below stay inside these ranges and needn't reach their ends.
Inputs may be any that keep to these rules, and one draw needn't show every extreme that they name: `counts`: 85 devices use all 2 slots, the others one; the used slots of a device come first. `rel_index`: entry (i, j) depends only on the offset between window positions i and j; distinct offsets have distinct entries. `region_ids`: nine rectangular regions of the shifted grid, separated by two row cuts and two column cuts; each id labels one region.
All inputs are finite; a program needn't handle non-finite values.
Results may differ from the reference program's by a relative error of at most 0.025.
Values may be sent and summed in bfloat16 or wider, within the bound.
No kernel may reach another device: no remote copies, remote signals or barrier semaphores. Data moves between devices by JAX's collectives and lax.ppermute only.
A program may use at most 192 MiB of HBM per device.

```python
import math
import jax
import jax.numpy as jnp
from jax import lax

HEADS = 16
WINDOW = 7
SIDE = 14
SHIFT = 3
LAYERS = 2
IMG_DEV = 2
C = 512
FF = 2048
TOKENS_IMG = 196
WIN_TOK = 49
TABLE = 169
IMAGES = 256
FULL_DEVICES = 85
DEVICES = 128


def draw_counts(key, part):
    shuffled = jax.random.permutation(key, DEVICES)
    return jnp.where(shuffled < FULL_DEVICES, IMG_DEV, 1).astype(jnp.int32)


def draw_rel_index(key, part):
    positions = jnp.arange(WIN_TOK)
    row_pos = positions // WINDOW
    col_pos = positions % WINDOW
    offsets = (row_pos[:, None] - row_pos[None, :] + WINDOW - 1) * (2 * WINDOW - 1) + (col_pos[:, None] - col_pos[None, :] + WINDOW - 1)
    shuffled = jax.random.permutation(key, TABLE)
    return shuffled[offsets].astype(jnp.int32)


def draw_region_ids(key, part):
    keys_all = jax.random.split(key, 5)
    row_first = jax.random.randint(keys_all[0], (), WINDOW - 2, WINDOW + 2)
    row_second = jax.random.randint(keys_all[1], (), SIDE - SHIFT - 1, SIDE - 1)
    col_first = jax.random.randint(keys_all[2], (), WINDOW - 2, WINDOW + 2)
    col_second = jax.random.randint(keys_all[3], (), SIDE - SHIFT - 1, SIDE - 1)
    positions = jnp.arange(SIDE)
    row_region = (positions >= row_first).astype(jnp.int32) + (positions >= row_second).astype(jnp.int32)
    col_region = (positions >= col_first).astype(jnp.int32) + (positions >= col_second).astype(jnp.int32)
    region = (3 * row_region[:, None] + col_region[None, :]).reshape(-1)
    relabel = jax.random.permutation(keys_all[4], 9)
    return relabel[region].astype(jnp.int32)


def draw_rel_table(key, part):
    normal_base = jnp.clip(jax.random.normal(jax.random.fold_in(key, 7), (LAYERS, TABLE, HEADS), jnp.float32), -4.0, 4.0)
    return normal_base.astype(jnp.bfloat16)


def spiked(values, rng, source, target, parts, factor):
    def block_of(dim):
        return (jnp.arange(values.shape[dim]) // (values.shape[dim] // parts)).reshape((-1,) + (1,) * (values.ndim - 1 - dim))

    near = jax.random.permutation(rng, parts)[block_of(target)]
    second = (block_of(target) + parts // 2) % parts
    return jnp.where((block_of(source) == near) | (block_of(source) == second), factor * values, values)


def steps_of(rng, dims, pieces, low, top_value):
    def one(axis_at, blocks):
        steps = jax.random.uniform(jax.random.fold_in(jax.random.fold_in(rng, 6), axis_at), (blocks,), jnp.float32, low / len(pieces), top_value / len(pieces))
        return jnp.repeat(jnp.exp(steps), dims[axis_at] // blocks).reshape((-1,) + (1,) * (len(dims) - axis_at - 1))

    level = one(*pieces[0])
    for cut in pieces[1:]:
        level = level * one(*cut)
    return level


def centred(stream_key, shape, width, most, cuts=(), held_as=jnp.bfloat16):
    array = width * jax.random.normal(stream_key, shape, jnp.float32)
    if cuts:
        array = array * steps_of(stream_key, shape, cuts, -0.22, 0.18)
    return jnp.clip(array, -most, most).astype(held_as)


def noise_with(own_key, extent, scale, bound, pieces, heavy, held_as=jnp.bfloat16):
    values = scale * jax.random.normal(own_key, extent, jnp.float32)
    if pieces:
        values = values * steps_of(own_key, extent, pieces, -0.22, 0.18)
    return jnp.clip(spiked(values, jax.random.fold_in(own_key, 3), *heavy), -bound, bound).astype(held_as)


def setup_inputs(seed: int = 0) -> dict:
    key_of = jax.random.split(jax.random.key(seed), 17)
    images = centred(key_of[0], (IMAGES, TOKENS_IMG, C), 1.0, 6.0, ((0, 128),))
    cotangent = noise_with(key_of[1], (IMAGES, TOKENS_IMG, C), 1.0, 24.0, ((0, 128),), (0, 2, 128, 5.5))
    counts = draw_counts(jax.random.fold_in(key_of[16], 71), 0)
    rel_index = draw_rel_index(jax.random.fold_in(key_of[16], 71), 0)
    region_ids = draw_region_ids(jax.random.fold_in(key_of[16], 71), 0)
    qkv_weight = centred(key_of[5], (LAYERS, C, 3 * C), C ** -0.5, 0.25, ((1, 16),))
    qv_bias = centred(key_of[6], (LAYERS, 2 * C), 0.5, 3.0, ((1, 16),))
    proj_weight = centred(key_of[7], (LAYERS, C, C), (C // 16) ** -0.5, 1.0, ((1, 16),))
    proj_bias = centred(key_of[8], (LAYERS, C), 0.5, 3.0, ((1, 16),))
    fc1_weight = centred(key_of[9], (LAYERS, C, FF), C ** -0.5, 0.25, ((1, 16),))
    fc1_bias = centred(key_of[10], (LAYERS, FF), 0.5, 3.0, ((1, 16),))
    fc2_weight = centred(key_of[11], (LAYERS, FF, C), FF ** -0.5, 0.125, ((1, 16),))
    fc2_bias = centred(key_of[12], (LAYERS, C), 0.5, 3.0, ((1, 16),))
    norm_gains = jnp.clip(1.0 + 0.1 * jax.random.normal(key_of[13], (LAYERS, 2, C), jnp.float32), 0.5, 1.5).astype(jnp.bfloat16)
    norm_biases = centred(key_of[14], (LAYERS, 2, C), 0.5, 3.0, ((2, 16),))
    rel_table = draw_rel_table(jax.random.fold_in(key_of[16], 71), 0)
    return {"images": images, "cotangent": cotangent, "counts": counts, "rel_index": rel_index, "region_ids": region_ids, "qkv_weight": qkv_weight, "qv_bias": qv_bias, "proj_weight": proj_weight, "proj_bias": proj_bias, "fc1_weight": fc1_weight, "fc1_bias": fc1_bias, "fc2_weight": fc2_weight, "fc2_bias": fc2_bias, "norm_gains": norm_gains, "norm_biases": norm_biases, "rel_table": rel_table}


EPS = 1e-05
MASKED = -1e+30
INV_ROOT2 = 0.7071067811865476
INV_ROOT_2PI = 0.3989422804014327

def product(pattern, first_op, second_op):
    return jnp.einsum(pattern, first_op.astype(jnp.float32), second_op.astype(jnp.float32))

def normalize(values, gain, offset):
    average = lax.optimization_barrier(jnp.mean(values, -1, keepdims=True))
    centered = values - average
    inv_std = lax.rsqrt(lax.optimization_barrier(jnp.mean(centered * centered, -1, keepdims=True)) + EPS)
    unit_val = centered * inv_std
    return (unit_val * gain + offset, unit_val, inv_std)

def normalize_back(upstream, unit_val, inv_std, gain):
    d_unit = upstream * gain
    result = inv_std * (d_unit - lax.optimization_barrier(jnp.mean(d_unit, -1, keepdims=True)) - unit_val * lax.optimization_barrier(jnp.mean(d_unit * unit_val, -1, keepdims=True)))
    return (result, lax.optimization_barrier(jnp.sum(upstream * unit_val, 0)), lax.optimization_barrier(jnp.sum(upstream, 0)))

def gelu_value(hidden):
    return 0.5 * hidden * (1.0 + jax.scipy.special.erf(hidden * INV_ROOT2))

def gelu_slope(hidden):
    return 0.5 * (1.0 + jax.scipy.special.erf(hidden * INV_ROOT2)) + hidden * jnp.exp(-0.5 * hidden * hidden) * INV_ROOT_2PI

def to_windows(tensor, shifted):
    n_images = tensor.shape[0]
    channels = tensor.shape[-1]
    per_side = SIDE // WINDOW
    grid_view = tensor.reshape(n_images, SIDE, SIDE, channels)
    if shifted:
        grid_view = jnp.roll(grid_view, (-SHIFT, -SHIFT), (1, 2))
    grid_view = grid_view.reshape(n_images, per_side, WINDOW, per_side, WINDOW, channels).transpose(0, 1, 3, 2, 4, 5)
    return grid_view.reshape(n_images * per_side * per_side, WIN_TOK, channels)

def from_windows(windows, shifted):
    per_side = SIDE // WINDOW
    n_images = windows.shape[0] // (per_side * per_side)
    channels = windows.shape[-1]
    grid_view = windows.reshape(n_images, per_side, per_side, WINDOW, WINDOW, channels).transpose(0, 1, 3, 2, 4, 5)
    grid_view = grid_view.reshape(n_images, SIDE, SIDE, channels)
    if shifted:
        grid_view = jnp.roll(grid_view, (SHIFT, SHIFT), (1, 2))
    return grid_view.reshape(n_images, TOKENS_IMG, channels)

def split_heads(tokens_f, shifted, n_heads):
    n_images = tokens_f.shape[0] // TOKENS_IMG
    windows = to_windows(tokens_f.reshape(n_images, TOKENS_IMG, -1), shifted)
    return windows.reshape(windows.shape[0], WIN_TOK, n_heads, -1)

def merge_heads(windows, shifted):
    merged = from_windows(windows.reshape(windows.shape[0], WIN_TOK, -1), shifted)
    return merged.reshape(-1, merged.shape[-1])

def masked_scores(query_win, key_win, pos_bias, allowed):
    scores = product('wqhd,wkhd->whqk', query_win, key_win) + pos_bias[None]
    if allowed is not None:
        per_image = allowed.shape[0]
        full_shape = scores.shape
        grouped = scores.reshape(full_shape[0] // per_image, per_image, full_shape[1], full_shape[2], full_shape[3])
        scores = jnp.where(allowed[None, :, None], grouped, MASKED).reshape(full_shape)
    return scores

def layer_forward(tokens_f, weights, shifted, pos_bias, allowed):
    mix_w, mix_b, out_w, out_b, up_w, up_b, down_w, down_b, norm_gain, norm_shift, pos_table = weights
    feat_dim = mix_w.shape[0]
    n_heads = pos_table.shape[1]
    q_scale = (feat_dim // n_heads) ** (-0.5)
    gain_f = norm_gain.astype(jnp.float32)
    shift_f = norm_shift.astype(jnp.float32)
    normed, unit_one, rstd_one = normalize(tokens_f, gain_f[0], shift_f[0])
    normed_one = normed.astype(jnp.bfloat16)
    mixed_out = product('tc,cf->tf', normed_one, mix_w)
    bias_f = mix_b.astype(jnp.float32)
    queries = ((mixed_out[:, :feat_dim] + bias_f[:feat_dim]) * q_scale).astype(jnp.bfloat16)
    key_rows = mixed_out[:, feat_dim:2 * feat_dim].astype(jnp.bfloat16)
    values = (mixed_out[:, 2 * feat_dim:] + bias_f[feat_dim:]).astype(jnp.bfloat16)
    query_win = split_heads(queries, shifted, n_heads)
    key_win = split_heads(key_rows, shifted, n_heads)
    value_win = split_heads(values, shifted, n_heads)
    scores = masked_scores(query_win, key_win, pos_bias, allowed)
    row_max = lax.optimization_barrier(jnp.max(scores, -1, keepdims=True))
    log_total = row_max + jnp.log(lax.optimization_barrier(jnp.sum(jnp.exp(scores - row_max), -1, keepdims=True)))
    prob_bf = jnp.exp(scores - log_total).astype(jnp.bfloat16)
    attended = merge_heads(product('whqk,wkhd->wqhd', prob_bf, value_win), shifted).astype(jnp.bfloat16)
    residual = tokens_f + product('tc,ce->te', attended, out_w) + out_b.astype(jnp.float32)
    normed, unit_two, rstd_two = normalize(residual, gain_f[1], shift_f[1])
    normed_two = normed.astype(jnp.bfloat16)
    hidden = product('tc,cf->tf', normed_two, up_w) + up_b.astype(jnp.float32)
    act_bf = gelu_value(hidden).astype(jnp.bfloat16)
    result = residual + product('tf,fc->tc', act_bf, down_w) + down_b.astype(jnp.float32)
    saved = (unit_one, rstd_one, normed_one, query_win, key_win, value_win, log_total, attended, unit_two, rstd_two, normed_two, hidden, act_bf)
    return (result, saved)

def layer_backward(gradient, saved, weights, shifted, pos_bias, allowed, fold_bias):
    mix_w, mix_b, out_w, out_b, up_w, up_b, down_w, down_b, norm_gain, norm_shift, pos_table = weights
    unit_one, rstd_one, normed_one, query_win, key_win, value_win, log_total, attended, unit_two, rstd_two, normed_two, hidden, act_bf = saved
    feat_dim = mix_w.shape[0]
    n_heads = pos_table.shape[1]
    q_scale = (feat_dim // n_heads) ** (-0.5)
    gain_f = norm_gain.astype(jnp.float32)
    down_b_grad = lax.optimization_barrier(jnp.sum(gradient, 0))
    grad_bf = gradient.astype(jnp.bfloat16)
    down_w_grad = product('tf,tc->fc', act_bf, grad_bf)
    grad_hidden = product('tc,fc->tf', grad_bf, down_w) * gelu_slope(hidden)
    up_b_grad = lax.optimization_barrier(jnp.sum(grad_hidden, 0))
    hidden_bf = grad_hidden.astype(jnp.bfloat16)
    up_w_grad = product('tc,tf->cf', normed_two, hidden_bf)
    grad_normed = product('tf,cf->tc', hidden_bf, up_w)
    back_two, gain_two_grad, shift_two_grad = normalize_back(grad_normed, unit_two, rstd_two, gain_f[1])
    grad_resid = gradient + back_two
    out_b_grad = lax.optimization_barrier(jnp.sum(grad_resid, 0))
    resid_bf = grad_resid.astype(jnp.bfloat16)
    out_w_grad = product('tc,te->ce', attended, resid_bf)
    grad_attended = product('te,ce->tc', resid_bf, out_w).astype(jnp.bfloat16)
    attended_win = split_heads(grad_attended, shifted, n_heads)
    scores = masked_scores(query_win, key_win, pos_bias, allowed)
    attn_prob = jnp.exp(scores - log_total)
    grad_probs = product('wqhd,wkhd->whqk', attended_win, value_win)
    grad_values = product('whqk,wqhd->wkhd', attn_prob.astype(jnp.bfloat16), attended_win)
    grad_scores = attn_prob * (grad_probs - lax.optimization_barrier(jnp.sum(attn_prob * grad_probs, -1, keepdims=True)))
    table_grad = fold_bias(lax.optimization_barrier(jnp.sum(grad_scores, 0)))
    scores_bf = grad_scores.astype(jnp.bfloat16)
    grad_queries = merge_heads(product('whqk,wkhd->wqhd', scores_bf, key_win) * q_scale, shifted)
    grad_keys = merge_heads(product('whqk,wqhd->wkhd', scores_bf, query_win), shifted)
    grad_values = merge_heads(grad_values, shifted)
    mix_b_grad = jnp.concatenate([lax.optimization_barrier(jnp.sum(grad_queries, 0)), lax.optimization_barrier(jnp.sum(grad_values, 0))])
    mixed_bf = jnp.concatenate([grad_queries, grad_keys, grad_values], -1).astype(jnp.bfloat16)
    mix_w_grad = product('tc,tf->cf', normed_one, mixed_bf)
    grad_normed = product('tf,cf->tc', mixed_bf, mix_w)
    back_one, gain_one_grad, shift_one_grad = normalize_back(grad_normed, unit_one, rstd_one, gain_f[0])
    grads = (mix_w_grad, mix_b_grad, out_w_grad, out_b_grad, up_w_grad, up_b_grad, down_w_grad, down_b_grad, jnp.stack([gain_one_grad, gain_two_grad]), jnp.stack([shift_one_grad, shift_two_grad]), table_grad)
    return (grad_resid + back_one, grads)

def reference(images, cotangent, counts, rel_index, region_ids, qkv_weight, qv_bias, proj_weight, proj_bias, fc1_weight, fc1_bias, fc2_weight, fc2_bias, norm_gains, norm_biases, rel_table):
    params = (qkv_weight, qv_bias, proj_weight, proj_bias, fc1_weight, fc1_bias, fc2_weight, fc2_bias, norm_gains, norm_biases, rel_table)
    slot_ids = jnp.arange(IMAGES)
    live_mask = (slot_ids % IMG_DEV < counts[slot_ids // IMG_DEV]).astype(jnp.float32)
    ids_win = to_windows(region_ids.reshape(1, TOKENS_IMG, 1), False)[:, :, 0]
    allowed = ids_win[:, :, None] == ids_win[:, None, :]
    pos_biases = [rel_table[layer_id].astype(jnp.float32)[rel_index].transpose(2, 0, 1) for layer_id in range(LAYERS)]

    def fold_bias(grad_bias):
        flat_bias = grad_bias.transpose(1, 2, 0).reshape(WIN_TOK * WIN_TOK, -1)
        return jax.ops.segment_sum(flat_bias, rel_index.reshape(-1), num_segments=TABLE)
    step_images = math.gcd(IMAGES, 16)
    n_blocks = IMAGES // step_images

    def block_step(totals, block_in):
        img_block, cot_block, live_block = block_in
        tokens_f = img_block.astype(jnp.float32).reshape(-1, C)
        saved_all = []
        for layer_id in range(LAYERS):
            weights = tuple((p[layer_id] for p in params))
            shifted = layer_id % 2 == 1
            tokens_f, saved = layer_forward(tokens_f, weights, shifted, pos_biases[layer_id], allowed if shifted else None)
            saved_all.append(saved)
        row_mask = jnp.repeat(live_block, TOKENS_IMG)[:, None]
        result = tokens_f * row_mask
        gradient = cot_block.astype(jnp.float32).reshape(-1, C) * row_mask
        for layer_id in reversed(range(LAYERS)):
            weights = tuple((p[layer_id] for p in params))
            shifted = layer_id % 2 == 1
            gradient, grads = layer_backward(gradient, saved_all[layer_id], weights, shifted, pos_biases[layer_id], allowed if shifted else None, fold_bias)
            totals = tuple((t.at[layer_id].add(g) for t, g in zip(totals, grads)))
        return (totals, (result.reshape(step_images, TOKENS_IMG, C), gradient.reshape(step_images, TOKENS_IMG, C)))
    zero_sums = tuple((jnp.zeros(p.shape, jnp.float32) for p in params))
    inputs = (images.reshape(n_blocks, step_images, TOKENS_IMG, C), cotangent.reshape(n_blocks, step_images, TOKENS_IMG, C), live_mask.reshape(n_blocks, step_images))
    totals, (results, gradients) = lax.scan(block_step, zero_sums, inputs)
    return (results.reshape(IMAGES, TOKENS_IMG, C), gradients.reshape(IMAGES, TOKENS_IMG, C), totals[0], totals[1], totals[2], totals[3], totals[4], totals[5], totals[6], totals[7], totals[8], totals[9], totals[10])
```

```python
import jax
import jax.numpy as jnp
from jax import lax
from jax.experimental import pallas as pl
from jax.experimental.pallas import tpu as pltpu
from jax.sharding import PartitionSpec as P

WINDOW = 7
SIDE = 14
SHIFT = 3
LAYERS = 2
TOKENS_IMG = 196
WIN_TOK = 49
TABLE = 169


EPS = 1e-05
MASKED = -1e30
INV_ROOT2 = 0.7071067811865476
INV_ROOT_2PI = 0.3989422804014327


def product(pattern, first_op, second_op):
    return jnp.einsum(pattern, first_op, second_op, preferred_element_type=jnp.float32)


def normalize(values, gain, offset):
    average = jnp.mean(values, -1, keepdims=True)
    centered = values - average
    inv_std = lax.rsqrt(jnp.mean(centered * centered, -1, keepdims=True) + EPS)
    unit_val = centered * inv_std
    return (unit_val * gain + offset, unit_val, inv_std)


def normalize_back(upstream, unit_val, inv_std, gain):
    d_unit = upstream * gain
    result = inv_std * (
        d_unit
        - jnp.mean(d_unit, -1, keepdims=True)
        - unit_val * jnp.mean(d_unit * unit_val, -1, keepdims=True)
    )
    return (result, jnp.sum(upstream * unit_val, 0), jnp.sum(upstream, 0))


def gelu_value(hidden):
    return 0.5 * hidden * (1.0 + jax.scipy.special.erf(hidden * INV_ROOT2))


def gelu_slope(hidden):
    return (
        0.5 * (1.0 + jax.scipy.special.erf(hidden * INV_ROOT2))
        + hidden * jnp.exp(-0.5 * hidden * hidden) * INV_ROOT_2PI
    )


def to_windows(tensor, shifted):
    n_images = tensor.shape[0]
    channels = tensor.shape[-1]
    per_side = SIDE // WINDOW
    grid_view = tensor.reshape(n_images, SIDE, SIDE, channels)
    if shifted:
        grid_view = jnp.roll(grid_view, (-SHIFT, -SHIFT), (1, 2))
    grid_view = grid_view.reshape(n_images, per_side, WINDOW, per_side, WINDOW, channels).transpose(
        0, 1, 3, 2, 4, 5
    )
    return grid_view.reshape(n_images * per_side * per_side, WIN_TOK, channels)


def from_windows(windows, shifted):
    per_side = SIDE // WINDOW
    n_images = windows.shape[0] // (per_side * per_side)
    channels = windows.shape[-1]
    grid_view = windows.reshape(n_images, per_side, per_side, WINDOW, WINDOW, channels).transpose(
        0, 1, 3, 2, 4, 5
    )
    grid_view = grid_view.reshape(n_images, SIDE, SIDE, channels)
    if shifted:
        grid_view = jnp.roll(grid_view, (SHIFT, SHIFT), (1, 2))
    return grid_view.reshape(n_images, TOKENS_IMG, channels)


def split_heads(tokens_f, shifted, n_heads):
    n_images = tokens_f.shape[0] // TOKENS_IMG
    windows = to_windows(tokens_f.reshape(n_images, TOKENS_IMG, -1), shifted)
    return windows.reshape(windows.shape[0], WIN_TOK, n_heads, -1)


def merge_heads(windows, shifted):
    merged = from_windows(windows.reshape(windows.shape[0], WIN_TOK, -1), shifted)
    return merged.reshape(-1, merged.shape[-1])


def masked_scores(query_win, key_win, pos_bias, allowed):
    scores = product("wqhd,wkhd->whqk", query_win, key_win) + pos_bias[None]
    if allowed is not None:
        per_image = allowed.shape[0]
        full_shape = scores.shape
        grouped = scores.reshape(
            full_shape[0] // per_image, per_image, full_shape[1], full_shape[2], full_shape[3]
        )
        scores = jnp.where(allowed[None, :, None], grouped, MASKED).reshape(full_shape)
    return scores


def layer_forward(tokens_f, weights, shifted, pos_bias, allowed):
    mix_w, mix_b, out_w, out_b, up_w, up_b, down_w, down_b, norm_gain, norm_shift, pos_table = (
        weights
    )
    feat_dim = mix_w.shape[0]
    n_heads = pos_table.shape[1]
    q_scale = (feat_dim // n_heads) ** (-0.5)
    gain_f = norm_gain.astype(jnp.float32)
    shift_f = norm_shift.astype(jnp.float32)
    normed, unit_one, rstd_one = normalize(tokens_f, gain_f[0], shift_f[0])
    normed_one = normed.astype(jnp.bfloat16)
    mixed_out = product("tc,cf->tf", normed_one, mix_w)
    bias_f = mix_b.astype(jnp.float32)
    queries = ((mixed_out[:, :feat_dim] + bias_f[:feat_dim]) * q_scale).astype(jnp.bfloat16)
    key_rows = mixed_out[:, feat_dim : 2 * feat_dim].astype(jnp.bfloat16)
    values = (mixed_out[:, 2 * feat_dim :] + bias_f[feat_dim:]).astype(jnp.bfloat16)
    query_win = split_heads(queries, shifted, n_heads)
    key_win = split_heads(key_rows, shifted, n_heads)
    value_win = split_heads(values, shifted, n_heads)
    scores = masked_scores(query_win, key_win, pos_bias, allowed)
    row_max = jnp.max(scores, -1, keepdims=True)
    log_total = row_max + jnp.log(jnp.sum(jnp.exp(scores - row_max), -1, keepdims=True))
    prob_bf = jnp.exp(scores - log_total).astype(jnp.bfloat16)
    attended = merge_heads(product("whqk,wkhd->wqhd", prob_bf, value_win), shifted).astype(
        jnp.bfloat16
    )
    residual = tokens_f + product("tc,ce->te", attended, out_w) + out_b.astype(jnp.float32)
    normed, unit_two, rstd_two = normalize(residual, gain_f[1], shift_f[1])
    normed_two = normed.astype(jnp.bfloat16)
    hidden = product("tc,cf->tf", normed_two, up_w) + up_b.astype(jnp.float32)
    act_bf = gelu_value(hidden).astype(jnp.bfloat16)
    result = residual + product("tf,fc->tc", act_bf, down_w) + down_b.astype(jnp.float32)
    saved = (
        unit_one,
        rstd_one,
        normed_one,
        query_win,
        key_win,
        value_win,
        log_total,
        attended,
        unit_two,
        rstd_two,
        normed_two,
        hidden,
        act_bf,
    )
    return (result, saved)


def layer_backward(gradient, saved, weights, shifted, pos_bias, allowed, fold_bias):
    mix_w, mix_b, out_w, out_b, up_w, up_b, down_w, down_b, norm_gain, norm_shift, pos_table = (
        weights
    )
    (
        unit_one,
        rstd_one,
        normed_one,
        query_win,
        key_win,
        value_win,
        log_total,
        attended,
        unit_two,
        rstd_two,
        normed_two,
        hidden,
        act_bf,
    ) = saved
    feat_dim = mix_w.shape[0]
    n_heads = pos_table.shape[1]
    q_scale = (feat_dim // n_heads) ** (-0.5)
    gain_f = norm_gain.astype(jnp.float32)
    down_b_grad = jnp.sum(gradient, 0)
    grad_bf = gradient.astype(jnp.bfloat16)
    grad_hidden = product("tc,fc->tf", grad_bf, down_w) * gelu_slope(hidden)
    up_b_grad = jnp.sum(grad_hidden, 0)
    hidden_bf = grad_hidden.astype(jnp.bfloat16)
    grad_normed = product("tf,cf->tc", hidden_bf, up_w)
    back_two, gain_two_grad, shift_two_grad = normalize_back(
        grad_normed, unit_two, rstd_two, gain_f[1]
    )
    grad_resid = gradient + back_two
    out_b_grad = jnp.sum(grad_resid, 0)
    resid_bf = grad_resid.astype(jnp.bfloat16)
    grad_attended = product("te,ce->tc", resid_bf, out_w).astype(jnp.bfloat16)
    attended_win = split_heads(grad_attended, shifted, n_heads)
    scores = masked_scores(query_win, key_win, pos_bias, allowed)
    attn_prob = jnp.exp(scores - log_total)
    grad_probs = product("wqhd,wkhd->whqk", attended_win, value_win)
    grad_values = product("whqk,wqhd->wkhd", attn_prob.astype(jnp.bfloat16), attended_win)
    grad_scores = attn_prob * (grad_probs - jnp.sum(attn_prob * grad_probs, -1, keepdims=True))
    table_grad = fold_bias(jnp.sum(grad_scores, 0))
    scores_bf = grad_scores.astype(jnp.bfloat16)
    grad_queries = merge_heads(product("whqk,wkhd->wqhd", scores_bf, key_win) * q_scale, shifted)
    grad_keys = merge_heads(product("whqk,wqhd->wkhd", scores_bf, query_win), shifted)
    grad_values = merge_heads(grad_values, shifted)
    mix_b_grad = jnp.concatenate([jnp.sum(grad_queries, 0), jnp.sum(grad_values, 0)])
    mixed_bf = jnp.concatenate([grad_queries, grad_keys, grad_values], -1).astype(jnp.bfloat16)
    grad_normed = product("tf,cf->tc", mixed_bf, mix_w)
    back_one, gain_one_grad, shift_one_grad = normalize_back(
        grad_normed, unit_one, rstd_one, gain_f[0]
    )
    factors = (
        (normed_one, mixed_bf),
        (attended, resid_bf),
        (normed_two, hidden_bf),
        (act_bf, grad_bf),
    )
    mix_w_grad = product("tc,tf->cf", normed_one, mixed_bf)
    out_w_grad = product("tc,te->ce", attended, resid_bf)
    up_w_grad = product("tc,tf->cf", normed_two, hidden_bf)
    down_w_grad = product("tf,tc->fc", act_bf, grad_bf)
    grads = (
        mix_w_grad,
        mix_b_grad,
        out_w_grad,
        out_b_grad,
        up_w_grad,
        up_b_grad,
        down_w_grad,
        down_b_grad,
        jnp.stack([gain_one_grad, gain_two_grad]),
        jnp.stack([shift_one_grad, shift_two_grad]),
        table_grad,
    )
    return (grad_resid + back_one, grads, factors)


FSDP_PAIRS = (
    [(f, f ^ 4) for f in range(16)],
    [(f, (3 - f // 4) * 4 + f % 4) for f in range(16)],
    [(f, f ^ 1) for f in range(16)],
    [(f, f // 4 * 4 + 3 - f % 4) for f in range(16)],
)
X_PAIRS = ([(d, d ^ 2) for d in range(8)], [(d, (3 - d // 2) * 2 + d % 2) for d in range(8)])
CORE_PAIRS = [(d, d ^ 1) for d in range(8)]
ORDERS = ((0, 1, 2, 3), (1, 0, 3, 2), (2, 3, 0, 1), (3, 2, 1, 0))
LANES = 128
SMALL = 16
ROWS = 192
SHARES = 16


def group_rows(group):
    return ROWS + SMALL if group == 0 else ROWS


def my_place():
    share = lax.axis_index("fsdp")
    core = lax.axis_index("dp") % 2
    z_at, y_at = share // 4, share % 4
    z_v, y_v = z_at // 2, y_at // 2
    bits = [(z_at + z_v) % 2, z_v, (y_at + y_v) % 2, y_v]
    return jnp.stack(bits + [core]).astype(jnp.int32)


def share_at(place, group, slot):
    bits = [None] * 4
    for at, bit in enumerate(ORDERS[group]):
        own = place[bit]
        bits[bit] = 1 - own if (slot >> (3 - at)) & 1 else own
    z_low = jnp.where(bits[0] == bits[1], 0, 1)
    y_low = jnp.where(bits[2] == bits[3], 0, 1)
    return (bits[1] * 2 + z_low) * 4 + bits[3] * 2 + y_low


def chunk_place(chunk, group):
    at = group * LANES
    if chunk < 3:
        return (0, 0, chunk * 512 + at)
    if chunk == 3:
        return (1, 0, at)
    if chunk < 8:
        return (2, 0, (chunk - 4) * 512 + at)
    return (3, (chunk - 8) * 32, at)


def pack_small(parts):
    rows = []
    for part in parts:
        lead = part.shape[0]
        width = part.shape[-1]
        for low in range(0, width, LANES):
            piece = part[:, low : low + LANES]
            rows.append(jnp.pad(piece, ((0, 0), (0, LANES - piece.shape[1]))))
    while len(rows) < SMALL:
        rows.append(jnp.zeros((lead, LANES), rows[0].dtype))
    return jnp.stack(rows, 1)


def gather_parts(qkv, proj, fc1, fc2, small):
    core = lax.axis_index("dp") % 2
    chunks = [qkv[:, 0:512], qkv[:, 512:1024], qkv[:, 1024:], proj]
    chunks += [fc1[:, at * 512 : at * 512 + 512] for at in range(4)]
    chunks += [fc2[at * 32 : at * 32 + 32] for at in range(4)]
    even = jnp.concatenate(chunks[0::2], 0)
    odd = jnp.concatenate(chunks[1::2], 0)
    mine = jnp.where(core == 0, even, odd)
    bufs = []
    for group in range(4):
        piece = mine[:, group * LANES : (group + 1) * LANES]
        if group == 0:
            piece = jnp.concatenate([piece, small], 0)
        bufs.append(piece[None])
    return bufs


def gather_over_chips(bufs):
    firsts, seconds = [], []
    for step in range(4):
        for group in range(4):
            pairs = FSDP_PAIRS[ORDERS[group][3 - step]]
            other = lax.ppermute(bufs[group], "fsdp", pairs)
            if step < 3:
                bufs[group] = jnp.concatenate([bufs[group], other], 0)
            else:
                firsts.append(bufs[group])
                seconds.append(other)
    operands = []
    for group in range(4):
        operands += [
            firsts[group],
            seconds[group],
            lax.ppermute(firsts[group], "dp", CORE_PAIRS),
            lax.ppermute(seconds[group], "dp", CORE_PAIRS),
        ]
    return operands


def unpack_body(place, *refs):
    pieces, outs = refs[:16], refs[16:]
    first_core = place[4] == 0
    for group in range(4):
        for slot in range(16):
            share = share_at(place, group, slot)
            own_ref = pieces[group * 4 + slot // 8]
            other_ref = pieces[group * 4 + 2 + slot // 8]
            for step in range(6):
                rows = pl.ds(step * 32, 32)
                own = own_ref[slot % 8, rows, :]
                other = other_ref[slot % 8, rows, :]
                even = jnp.where(first_core, own, other)
                odd = jnp.where(first_core, other, own)
                for chunk, value in ((2 * step, even), (2 * step + 1, odd)):
                    out, row, lane = chunk_place(chunk, group)
                    outs[out][share, pl.ds(row, 32), pl.ds(lane, LANES)] = value
            if group == 0:
                outs[4][share] = own_ref[slot % 8, pl.ds(ROWS, SMALL), :]


def unpack_parts(place, operands):
    dtype = operands[0].dtype
    shapes = ((32, 1536), (32, 512), (32, 2048), (128, 512), (SMALL, LANES))
    outs = pl.pallas_call(
        unpack_body,
        in_specs=[pl.BlockSpec(memory_space=pltpu.SMEM)]
        + [pl.BlockSpec(memory_space=pltpu.VMEM)] * 16,
        out_specs=[pl.BlockSpec(memory_space=pltpu.VMEM)] * 5,
        out_shape=[jax.ShapeDtypeStruct((SHARES,) + shape, dtype) for shape in shapes],
        name="unpack_parts",
    )(place, *operands)
    return outs


def pack_body(place, qkv, proj, fc1, fc2, small, *outs):
    sources = (qkv, proj, fc1, fc2)
    first_core = place[4] == 0
    for group in range(4):
        for slot in range(16):
            share = share_at(place, group, slot)
            for step in range(6):
                values = []
                for chunk in (2 * step, 2 * step + 1):
                    source, row, lane = chunk_place(chunk, group)
                    values.append(sources[source][share, pl.ds(row, 32), pl.ds(lane, LANES)])
                own = jnp.where(first_core, values[0], values[1])
                other = jnp.where(first_core, values[1], values[0])
                rows = pl.ds(step * 32, 32)
                outs[group * 2][slot, rows, :] = own
                outs[group * 2 + 1][slot, rows, :] = other
            if group == 0:
                value = small[share]
                outs[0][slot, pl.ds(ROWS, SMALL), :] = value
                outs[1][slot, pl.ds(ROWS, SMALL), :] = value


def pack_grads(place, qkv, proj, fc1, fc2, small):
    shapes = [(SHARES, group_rows(group), LANES) for group in range(4) for _ in range(2)]
    return pl.pallas_call(
        pack_body,
        in_specs=[pl.BlockSpec(memory_space=pltpu.SMEM)]
        + [pl.BlockSpec(memory_space=pltpu.VMEM)] * 5,
        out_specs=[pl.BlockSpec(memory_space=pltpu.VMEM)] * 8,
        out_shape=[jax.ShapeDtypeStruct(shape, jnp.bfloat16) for shape in shapes],
        name="pack_grads",
    )(place, qkv, proj, fc1, fc2, small)


def add_rounded(first, second):
    return (first.astype(jnp.float32) + second.astype(jnp.float32)).astype(jnp.bfloat16)


def reduce_parts(packed):
    bufs = []
    for group in range(4):
        other = lax.ppermute(packed[group * 2 + 1], "dp", CORE_PAIRS)
        bufs.append(add_rounded(packed[group * 2], other))
    for step in range(4):
        half = 8 >> step
        for group in range(4):
            pairs = FSDP_PAIRS[ORDERS[group][step]]
            other = lax.ppermute(bufs[group][half:], "fsdp", pairs)
            bufs[group] = add_rounded(bufs[group][:half], other)
    joined = [
        jnp.concatenate([bufs[0][0], bufs[1][0]], 0),
        jnp.concatenate([bufs[2][0], bufs[3][0]], 0),
    ]
    for step in range(2):
        for at in range(2):
            other = lax.ppermute(joined[at], "dp", X_PAIRS[(step + at) % 2])
            joined[at] = add_rounded(joined[at], other)
    others = [lax.ppermute(joined[at], "dp", CORE_PAIRS) for at in range(2)]
    return joined + others


def finish_body(place, *refs):
    parts, outs = refs[: 4 * LAYERS], refs[4 * LAYERS :]
    first_core = place[4] == 0
    for layer_id in range(LAYERS):
        for group in range(4):
            base = 0 if group % 2 == 0 else group_rows(group - 1)
            own_ref = parts[layer_id * 4 + group // 2]
            other_ref = parts[layer_id * 4 + 2 + group // 2]
            for step in range(6):
                rows = pl.ds(base + step * 32, 32)
                own = own_ref[rows, :].astype(jnp.float32)
                other = other_ref[rows, :].astype(jnp.float32)
                even = jnp.where(first_core, own, other)
                odd = jnp.where(first_core, other, own)
                for chunk, value in ((2 * step, even), (2 * step + 1, odd)):
                    out, row, lane = chunk_place(chunk, group)
                    outs[out][layer_id, pl.ds(row, 32), pl.ds(lane, LANES)] = value
            if group == 0:
                outs[4][layer_id] = own_ref[pl.ds(ROWS, SMALL), :].astype(jnp.float32)


def finish_grads(place, parts):
    shapes = ((32, 1536), (32, 512), (32, 2048), (128, 512), (SMALL, LANES))
    return pl.pallas_call(
        finish_body,
        in_specs=[pl.BlockSpec(memory_space=pltpu.SMEM)]
        + [pl.BlockSpec(memory_space=pltpu.VMEM)] * (4 * LAYERS),
        out_specs=[pl.BlockSpec(memory_space=pltpu.VMEM)] * 5,
        out_shape=[jax.ShapeDtypeStruct((LAYERS,) + shape, jnp.float32) for shape in shapes],
        name="finish_grads",
    )(place, *parts)


def on_device(
    images,
    cotangent,
    counts,
    rel_index,
    region_ids,
    qkv_weight,
    qv_bias,
    proj_weight,
    proj_bias,
    fc1_weight,
    fc1_bias,
    fc2_weight,
    fc2_bias,
    norm_gains,
    norm_biases,
    rel_table,
):
    n_images = images.shape[0]
    feat_dim = images.shape[2]
    live_mask = (jnp.arange(n_images) < counts[0]).astype(jnp.float32)[:, None, None]
    onehot = (rel_index.reshape(-1)[:, None] == jnp.arange(TABLE)[None, :]).astype(jnp.float32)
    ids_win = to_windows(region_ids.reshape(1, TOKENS_IMG, 1), False)[:, :, 0]
    allowed = ids_win[:, :, None] == ids_win[:, None, :]

    def fold_bias(grad_bias):
        flat_bias = grad_bias.transpose(1, 2, 0).reshape(WIN_TOK * WIN_TOK, -1)
        return jnp.einsum("pr,ph->rh", onehot, flat_bias, precision=lax.Precision.HIGHEST)

    place = my_place()
    bufs_all = []
    for layer_id in range(LAYERS):
        small = pack_small(
            [
                qv_bias[layer_id][None],
                proj_bias[layer_id][None],
                fc1_bias[layer_id][None],
                fc2_bias[layer_id][None],
                norm_gains[layer_id, 0][None],
                norm_gains[layer_id, 1][None],
                norm_biases[layer_id, 0][None],
                norm_biases[layer_id, 1][None],
                rel_table[layer_id][:, 0][None],
            ]
        )[0]
        bufs_all.append(
            gather_parts(
                qkv_weight[layer_id],
                proj_weight[layer_id],
                fc1_weight[layer_id],
                fc2_weight[layer_id],
                small,
            )
        )
    weights_all = []
    pos_biases = []
    operands = None
    for layer_id in range(LAYERS):
        bufs = bufs_all[layer_id]
        if operands is not None:
            bufs, _ = lax.optimization_barrier((bufs, operands))
        operands = gather_over_chips(list(bufs))
        qkv_w, proj_w, fc1_w, fc2_w, small = unpack_parts(place, operands)
        weights_all.append(
            (
                qkv_w.reshape(512, 1536),
                small[:, 0, :64].reshape(-1),
                proj_w.reshape(512, 512),
                small[:, 1, :32].reshape(-1),
                fc1_w.reshape(512, 2048),
                small[:, 2].reshape(-1),
                fc2_w.reshape(2048, 512),
                small[:, 3, :32].reshape(-1),
                small[:, 4:6, :32].transpose(1, 0, 2).reshape(2, -1),
                small[:, 6:8, :32].transpose(1, 0, 2).reshape(2, -1),
                small[:, 8:10].reshape(SHARES, -1)[:, :TABLE].T,
            )
        )
    tokens_f = images.astype(jnp.float32).reshape(-1, feat_dim)
    saved_all = []
    for layer_id in range(LAYERS):
        weights = weights_all[layer_id]
        shifted = layer_id % 2 == 1
        gathered = jnp.einsum(
            "pr,rh->ph", onehot, weights[10].astype(jnp.float32), precision=lax.Precision.HIGHEST
        )
        pos_bias = gathered.reshape(WIN_TOK, WIN_TOK, -1).transpose(2, 0, 1)
        tokens_f, saved = layer_forward(
            tokens_f, weights, shifted, pos_bias, allowed if shifted else None
        )
        saved_all.append(saved)
        pos_biases.append(pos_bias)
    activations = tokens_f.reshape(n_images, TOKENS_IMG, feat_dim) * live_mask
    gradient = (cotangent.astype(jnp.float32) * live_mask).reshape(-1, feat_dim)
    parts_all = [None] * LAYERS
    for layer_id in reversed(range(LAYERS)):
        shifted = layer_id % 2 == 1
        gradient, grads, factors = layer_backward(
            gradient,
            saved_all[layer_id],
            weights_all[layer_id],
            shifted,
            pos_biases[layer_id],
            allowed if shifted else None,
            fold_bias,
        )
        small = pack_small(
            [
                grads[1].reshape(SHARES, -1),
                grads[3].reshape(SHARES, -1),
                grads[5].reshape(SHARES, -1),
                grads[7].reshape(SHARES, -1),
                grads[8][0].reshape(SHARES, -1),
                grads[8][1].reshape(SHARES, -1),
                grads[9][0].reshape(SHARES, -1),
                grads[9][1].reshape(SHARES, -1),
                grads[10].T,
            ]
        ).astype(jnp.bfloat16)
        packed = pack_grads(
            place,
            grads[0].astype(jnp.bfloat16).reshape(SHARES, 32, -1),
            grads[2].astype(jnp.bfloat16).reshape(SHARES, 32, -1),
            grads[4].astype(jnp.bfloat16).reshape(SHARES, 32, -1),
            grads[6].astype(jnp.bfloat16).reshape(SHARES, 128, -1),
            small,
        )
        parts_all[layer_id] = reduce_parts(packed)
    qkv_g, proj_g, fc1_g, fc2_g, small = finish_grads(place, sum(parts_all, []))
    return (
        activations,
        gradient.reshape(n_images, TOKENS_IMG, feat_dim),
        qkv_g,
        small[:, 0, :64],
        proj_g,
        small[:, 1, :32],
        fc1_g,
        small[:, 2],
        fc2_g,
        small[:, 3, :32],
        small[:, 4:6, :32],
        small[:, 6:8, :32],
        small[:, 8:10].reshape(LAYERS, -1)[:, :TABLE, None],
    )


def solution(mesh):
    return jax.shard_map(
        on_device,
        mesh=mesh,
        in_specs=(
            P(("dp", "fsdp"), None, None),
            P(("dp", "fsdp"), None, None),
            P(("dp", "fsdp")),
            P(),
            P(),
            P(None, "fsdp", None),
            P(None, "fsdp"),
            P(None, "fsdp", None),
            P(None, "fsdp"),
            P(None, "fsdp", None),
            P(None, "fsdp"),
            P(None, "fsdp", None),
            P(None, "fsdp"),
            P(None, None, "fsdp"),
            P(None, None, "fsdp"),
            P(None, None, "fsdp"),
        ),
        out_specs=(
            P(("dp", "fsdp"), None, None),
            P(("dp", "fsdp"), None, None),
            P(None, "fsdp", None),
            P(None, "fsdp"),
            P(None, "fsdp", None),
            P(None, "fsdp"),
            P(None, "fsdp", None),
            P(None, "fsdp"),
            P(None, "fsdp", None),
            P(None, "fsdp"),
            P(None, None, "fsdp"),
            P(None, None, "fsdp"),
            P(None, None, "fsdp"),
        ),
        check_vma=False,
    )
```
